128 devices in a mesh: depth: 16 (over x, y), au: 4 (over z_lo, core), vert: 2 (over z_hi).
Axes of the slice: x: 4, y: 4, z: 4 (z_hi: 2, z_lo: 2; z = z_hi * 2 + z_lo), core: 2. Of those that a mesh axis runs over, the one named last changes fastest.
Arguments:
- density: float32 [256, 512, 256], P('depth', 'au', 'vert'), may hold values from 0.3 to 3
- image_cotangent: float32 [2, 512, 256], P(None, 'au', 'vert'), may hold values from -6 to 6
- shear_rows: int32 [256], P('depth'), may hold values from -16 to 16, as said below
- shear_cols: int32 [256], P('depth'), may hold values from -16 to 16, as said below
- velocity_code: int32 [2, 256, 512, 256], P(None, 'depth', 'au', 'vert'), may hold values from 0 to 26
- limiter: int32 [2, 256, 512, 256], P(None, 'depth', 'au', 'vert'), may hold values 0 or 1
Outputs:
- density_cotangent: float32 [256, 512, 256], P('depth', 'au', 'vert')
The draws below stay inside these ranges and needn't reach their ends.
Inputs may be any that keep to these rules, and one draw needn't show every extreme that they name: `shear_rows`: both values -16 and 16 occur in every draw. `shear_cols`: both values -16 and 16 occur in every draw.
All inputs are finite; a program needn't handle non-finite values. No bound on the sum of `limiter` on one device may be relied on, other than what follows from the above.
Results may differ from the reference program's by a relative error of at most 0.0003.
Values sent between devices are 32-bit elements; how exact they have to be, the bound alone decides.
No kernel may reach another device: no remote copies, remote signals or barrier semaphores. Data moves between devices by JAX's collectives and lax.ppermute only.
A program may use at most 64 MiB of HBM per device.

```python
import math
import jax
import jax.numpy as jnp
from jax import lax

SHEAR = 16
STEPS = 2
NZ = 256
NU = 512
NV = 256


def shear_ramp(key, flip):
    slices = jnp.arange(NZ, dtype=jnp.int32)
    ramp = slices * (2 * SHEAR + 1) // NZ - SHEAR
    jitter = jax.random.randint(key, (NZ,), -2, 3, dtype=jnp.int32)
    values = jnp.clip(ramp + jitter, -SHEAR, SHEAR)
    values = jnp.where(slices == 0, -SHEAR, jnp.where(slices == NZ - 1, SHEAR, values))
    return (values * flip).astype(jnp.int32)


def draw_shear_rows(key, part):
    return shear_ramp(jax.random.fold_in(key, 11), 1)


def draw_shear_cols(key, part):
    return shear_ramp(jax.random.fold_in(key, 23), -1)


def touch_ends(values, stream_key, least, high):
    index_at = [jax.random.randint(jax.random.fold_in(stream_key, axis), (), 0, length) for axis, length in enumerate(values.shape)]
    main_axis = values.shape.index(max(values.shape))
    next_to = index_at[:main_axis] + [(index_at[main_axis] + 1) % values.shape[main_axis]] + index_at[main_axis + 1:]
    return values.at[tuple(index_at)].set(least).at[tuple(next_to)].set(high)


def block_levels(rng, dims, pieces, low, largest):
    level = 1.0
    for position, shards_of in pieces:
        heights = jax.random.uniform(jax.random.fold_in(jax.random.fold_in(rng, 6), position), (shards_of,), jnp.float32, low / len(pieces), largest / len(pieces))
        level = level * jnp.repeat(jnp.exp(heights), dims[position] // shards_of).reshape((-1,) + (1,) * (len(dims) - 1 - position))
    return level


def normal_values(key, dims, scale, bound, shards=(), kind=jnp.bfloat16):
    gain = block_levels(key, dims, shards, -0.22, 0.18) if shards else 1.0
    entries = jax.random.normal(key, dims, jnp.float32) * scale * gain
    return jnp.minimum(jnp.maximum(entries, -bound), bound).astype(kind)


def setup_inputs(seed: int = 0) -> dict:
    key_list = jax.random.split(jax.random.key(seed), 7)
    density = jnp.clip(jnp.exp(math.log(3.0) - 2.3025851 * jax.random.uniform(key_list[0], (NZ, NU, NV), jnp.float32) ** block_levels(key_list[0], (NZ, NU, NV), ((0, 16), (1, 4), (2, 2)), -0.2, 0.2)), 0.3, 3.0)
    image_cotangent = normal_values(key_list[1], (2, NU, NV), 1.0, 6.0, ((1, 4), (2, 2)), jnp.float32)
    shear_rows = draw_shear_rows(jax.random.fold_in(key_list[6], 71), 0)
    shear_cols = draw_shear_cols(jax.random.fold_in(key_list[6], 71), 0)
    velocity_code = touch_ends(jax.random.randint(key_list[4], (STEPS, NZ, NU, NV), 0, 27), jax.random.fold_in(key_list[4], 1), 0, 26).astype(jnp.int32)
    limiter = touch_ends((jax.random.randint(key_list[5], (STEPS, NZ, NU, NV), 0, 4) < 1).astype(jnp.int32), jax.random.fold_in(key_list[5], 1), 0, 1)
    return dict(density=density, image_cotangent=image_cotangent, shear_rows=shear_rows, shear_cols=shear_cols, velocity_code=velocity_code, limiter=limiter)


OPTICAL = 1.7
FRACTIONS = (0.3, 0.6, 0.45)


def shear_take(volume, offsets, axis_dim):
    pads = [(0, 0), (0, 0), (0, 0)]
    pads[axis_dim] = (SHEAR, SHEAR)
    padded = jnp.pad(volume, pads)
    length = volume.shape[axis_dim]

    def sample(plane, offset):
        return lax.dynamic_slice_in_dim(plane, (SHEAR + offset).astype(jnp.int32), length, axis_dim - 1)

    return jax.vmap(sample)(padded, offsets)


def column_gradient(views, cotangent, delta):
    optical = delta * views
    running = jnp.cumsum(optical, axis=0)
    transmit = jnp.exp(-(running - optical))
    opacity = -jnp.expm1(-optical)
    weighted = transmit * opacity * views
    light_sum = jnp.cumsum(weighted, axis=0)
    later_light = light_sum[-1:] - light_sum
    return cotangent[None] * (transmit * (jnp.exp(-optical) * views + opacity / delta) - later_light)


def sweep(values, offset, axis_dim, frac, direction):
    pads = [(0, 0), (0, 0), (0, 0)]
    pads[axis_dim] = (2, 2)
    padded = jnp.pad(values, pads)
    length = values.shape[axis_dim]

    def moved(distance):
        return lax.slice_in_dim(padded, 2 + distance, 2 + distance + length, axis=axis_dim)

    result = None
    for candidate in (-1, 0, 1):
        value = (1.0 - frac) * moved(direction * candidate) + frac * moved(direction * (candidate + 1))
        result = value if result is None else jnp.where(offset == candidate, value, result)
    return result


def adjoint_push(values, offsets, direction):
    values = sweep(values, offsets[2], 2, FRACTIONS[2], direction)
    values = sweep(values, offsets[1], 1, FRACTIONS[1], direction)
    return sweep(values, offsets[0], 0, FRACTIONS[0], direction)


def reference(density, image_cotangent, shear_rows, shear_cols, velocity_code, limiter):
    delta = OPTICAL / NZ
    grad_rows = column_gradient(shear_take(density, shear_rows, 1), image_cotangent[0], delta)
    grad_cols = column_gradient(shear_take(density, shear_cols, 2), image_cotangent[1], delta)
    cotangent = shear_take(grad_rows, -shear_rows, 1) + shear_take(grad_cols, -shear_cols, 2)
    for index in range(STEPS - 1, -1, -1):
        code = velocity_code[index]
        offsets = (code % 3 - 1, (code // 3) % 3 - 1, code // 9 - 1)
        kept = 0.5 * (1 - limiter[index]).astype(jnp.float32) * cotangent
        hat_grad = cotangent - adjoint_push(kept, offsets, -1)
        cotangent = kept + adjoint_push(hat_grad, offsets, 1)
    return cotangent
```

```python
import functools
import jax
import jax.numpy as jnp
from jax import lax
from jax.experimental import pallas as pl
from jax.experimental.pallas import tpu as pltpu
from jax.sharding import PartitionSpec as P

SHEAR = 16
OPTICAL = 1.7
FZ, FU, FV = (0.3, 0.6, 0.45)
NZ, NU, NV = 16, 128, 128
PAD = 8
EXT = NU + 2 * PAD + 32 + 2 * PAD
S0 = NU + 2 * PAD
f32 = jnp.float32


def lanes(rows):
    return lax.broadcasted_iota(jnp.int32, (rows, NV), 1)


def rot(x, shift, axis=1):
    n = x.shape[axis]
    if isinstance(shift, int):
        shift = shift % n
        return x if shift == 0 else pltpu.roll(x, shift, axis)
    return pltpu.roll(x, lax.rem(shift + 2 * n, n), axis)


def half_is(rows, v):
    return lax.rem(lax.div(lanes(rows), 16), 2) == v


def edge_image(rows_of):
    group = lax.div(lanes(32), 32)
    image = rot(rows_of(0), 16)
    for k in range(1, 4):
        image = jnp.where(group == k, rot(rows_of(k), 32 * k + 16), image)
    return image


def pack_pair(even, odd, v):
    return jnp.where(half_is(32, v), even, rot(odd, jnp.where(v == 0, 16, -16)))


def odd_shift(v):
    return jnp.where(v == 1, -16, 16)


def pack_volume(read, write, v):
    def body(p, _):
        even = edge_image(lambda k: read(2 * p, 32 * k))
        odd = edge_image(lambda k: read(2 * p + 1, 32 * k))
        write(p, pack_pair(even, odd, v))
        return 0

    lax.fori_loop(0, NZ // 2, body, 0)


def pack_density_kernel(x, top, bot, vst):
    v = lax.axis_index("vert")
    top[...] = x[:, 0:SHEAR, :]
    bot[...] = x[:, NU - SHEAR : NU, :]

    def write(p, val):
        vst[p] = val

    pack_volume(lambda z, r: x[z, r : r + 32, :], write, v)


def pack_code_kernel(code, lim, top, bot, vst):
    v = lax.axis_index("vert")
    for i, ref in enumerate((code, lim)):
        for s in range(2):
            a = 2 * s + i
            top[a] = ref[s, :, 0:PAD, :]
            bot[a] = ref[s, :, NU - PAD : NU, :]

            def write(p, val, a=a):
                vst[a, p] = val

            pack_volume(lambda z, r, ref=ref, s=s: ref[s, z, r : r + 32, :], write, v)


def column_shift(own, other, s, z, t, v, lane):
    k = lax.div(t, 4)
    moved = rot(own, -s)
    extra = odd_shift(v) if z % 2 else 0
    partner = rot(other, -(32 * k + 16) - s + extra + 256)
    index = lane + s
    inside = (index >= 0) & (index < NV)
    take = jnp.where(v == 0, index, NV - 1 - index) >= NV
    return jnp.where(inside, moved, jnp.where(take, partner, jnp.zeros_like(moved)))


def fill_rows(ext, own, top, bot):
    ext[:, 0:SHEAR, :] = top[...]
    ext[:, SHEAR : SHEAR + NU, :] = own[...]
    ext[:, SHEAR + NU : 2 * SHEAR + NU, :] = bot[...]


def opacity_of(x):
    return x * (1.0 - x * (1 / 2) * (1.0 - x * (1 / 3) * (1.0 - x * (1 / 4) * (1.0 - x * (1 / 5) * (1.0 - x * (1 / 6))))))


def ray_kernel(delta, rows, cols, x, top, bot, vst, g, block, ext):
    v = lax.axis_index("vert")
    fill_rows(ext, x, top, bot)
    lane = lanes(8)

    def body(t, _):
        r0 = pl.multiple_of(8 * t, 8)
        s0 = pl.multiple_of(8 * lax.rem(t, 4), 8)
        through = [jnp.ones((8, NV), f32)] * 2
        light = [jnp.zeros((8, NV), f32)] * 2
        for z in range(NZ):
            own = x[z, pl.ds(r0, 8), :]
            views = (
                ext[z, pl.ds(SHEAR + rows[z] + r0, 8), :],
                column_shift(own, vst[z // 2, pl.ds(s0, 8), :], cols[z], z, t, v, lane),
            )
            for i in range(2):
                opacity = opacity_of(delta * views[i])
                light[i] = light[i] + through[i] * (opacity * views[i])
                after = 1.0 - opacity
                g[i, z, pl.ds(r0, 8), :] = (
                    through[i] * (after * views[i] + opacity * (1.0 / delta)) + light[i]
                )
                through[i] = through[i] * after
        for i in range(2):
            block[t, 2 * i] = through[i]
            block[t, 2 * i + 1] = light[i]
        return 0

    lax.fori_loop(0, NU // 8, body, 0)


def scan_kernel(devices, block, out):
    for i in range(2):
        reach = jnp.ones((8, NV), f32)
        reaches = []
        for d in range(devices):
            out[d, 2 * i] = reach
            reaches.append(reach)
            reach = reach * block[d, 2 * i]
        later = jnp.zeros((8, NV), f32)
        for d in range(devices - 1, -1, -1):
            out[d, 2 * i + 1] = later
            later = later + reaches[d] * block[d, 2 * i + 1]


def grad_kernel(g, block, far, image, vg, top, bot, vst):
    v = lax.axis_index("vert")

    def body(t, _):
        r0 = pl.multiple_of(8 * t, 8)
        for i in range(2):
            cot = image[i, pl.ds(r0, 8), :]
            scale = cot * far[t, 2 * i]
            base = scale * block[t, 2 * i + 1] + cot * far[t, 2 * i + 1]
            for z in range(NZ):
                vg[i, z, pl.ds(r0, 8), :] = scale * g[i, z, pl.ds(r0, 8), :] - base
        return 0

    lax.fori_loop(0, NU // 8, body, 0)
    top[...] = vg[0, :, 0:SHEAR, :]
    bot[...] = vg[0, :, NU - SHEAR : NU, :]

    def write(p, val):
        vst[p] = val

    pack_volume(lambda z, r: vg[1, z, r : r + 32, :], write, v)


def cotangent_kernel(rows, cols, vg, top, bot, vst, cot, ctop, cbot, cvst, ext):
    v = lax.axis_index("vert")
    fill_rows(ext, vg.at[0], top, bot)
    lane = lanes(8)

    def body(t, _):
        r0 = pl.multiple_of(8 * t, 8)
        s0 = pl.multiple_of(8 * lax.rem(t, 4), 8)
        for z in range(NZ):
            first = ext[z, pl.ds(SHEAR - rows[z] + r0, 8), :]
            second = column_shift(
                vg[1, z, pl.ds(r0, 8), :], vst[z // 2, pl.ds(s0, 8), :], -cols[z], z, t, v, lane
            )
            cot[z, pl.ds(r0, 8), :] = first + second
        return 0

    lax.fori_loop(0, NU // 8, body, 0)
    ctop[...] = cot[:, 0:PAD, :]
    cbot[...] = cot[:, NU - PAD : NU, :]

    def write(p, val):
        cvst[p] = val

    pack_volume(lambda z, r: cot[z, r : r + 32, :], write, v)


def assemble(read, tops, bots, partner, write, v):
    lane = lanes(8)
    near = (lane >= 64) == (v == 0)
    half = half_is(32, v)

    def body(p, _):
        for odd in range(2):
            z = 2 * p + odd
            own = edge_image(lambda k: read(z, 32 * k, 32))
            other = partner(p)
            if odd:
                other = rot(other, odd_shift(v))
            strip = jnp.where(half, own, other)
            top = tops[0](z)
            bot = bots[0](z)
            above = rot(jnp.where(near, top, tops[1](z)), 16)
            below = rot(jnp.where(near, bot, bots[1](z)), 112)
            write(z, 0, top)
            write(z, PAD, read(z, 0, NU))
            write(z, PAD + NU, bot)
            write(z, S0, jnp.where(lane < 32, above, rot(strip[24:32], 32)))
            write(z, S0 + PAD, strip)
            write(z, S0 + PAD + 32, jnp.where(lane >= 96, below, rot(strip[0:8], -32)))
        return 0

    lax.fori_loop(0, NZ // 2, body, 0)


def encode(code, lim):
    hi = code >= 18
    mid = code >= 9
    rest = code - jnp.where(mid, 9, 0) - jnp.where(hi, 9, 0)
    uhi = rest >= 6
    umid = rest >= 3
    last = rest - jnp.where(umid, 3, 0) - jnp.where(uhi, 3, 0)
    one = lambda m, b: jnp.where(m, b, 0)
    return (
        one(code < 9, 1) + one(hi, 2) + one(rest < 3, 4) + one(uhi, 8)
        + one(last == 0, 16) + one(last == 2, 32) + one(lim > 0, 64)
    )


def code_kernel(code, lim, top, bot, dtop, dbot, vst, out):
    v = lax.axis_index("vert")
    for s in range(2):
        pair = lambda ref, z, s=s: ref[2 * s, z] + 27 * ref[2 * s + 1, z]

        def write(z, r, val, s=s):
            lim_of = jnp.where(val >= 27, 1, 0)
            out[s, z, pl.ds(r, val.shape[0]), :] = encode(val - 27 * lim_of, lim_of)

        assemble(
            lambda z, r, n, s=s: code[s, z, pl.ds(r, n), :] + 27 * lim[s, z, pl.ds(r, n), :],
            (functools.partial(pair, top), functools.partial(pair, dtop)),
            (functools.partial(pair, bot), functools.partial(pair, dbot)),
            lambda p, s=s: vst[2 * s, p] + 27 * vst[2 * s + 1, p],
            write,
            v,
        )


def bit(m, b):
    return (m & b) != 0


def plane_sweeps(g, m, backward):
    lane = lanes(EXT)
    first, last = lane == 0, lane == NV - 1
    near, far = (first, last) if backward else (last, first)
    step = 1 if backward else -1
    fg = FV * g
    h = (1.0 - FV) * g + jnp.where(near, 0.0, rot(fg, step))
    ahead = jnp.where(far, fg, rot(h, -step))
    behind = jnp.where(near, 0.0, rot(h, step))
    g = jnp.where(bit(m, 1), ahead, jnp.where(bit(m, 2), behind, h))
    h = (1.0 - FU) * g + FU * rot(g, step, 0)
    return jnp.where(bit(m, 4), rot(h, -step, 0), jnp.where(bit(m, 8), rot(h, step, 0), h))


def kept_of(cot, m):
    return jnp.where(bit(m, 64), 0.0, 0.5 * cot)


ROWS = 16


def depth_sweep(g, below, above, m, backward, emit):
    def body(t, _):
        r = pl.ds(pl.multiple_of(ROWS * t, ROWS), ROWS)
        nb, na = below.shape[0], above.shape[0]

        def at(z):
            if z < 0:
                return below[nb + z, r, :]
            if z >= NZ:
                return above[z - NZ, r, :]
            return g[z, r, :]

        prev = -1 if backward else 1

        def h(z):
            return (1.0 - FZ) * at(z) + FZ * at(z + prev)

        window = [h(-1), h(0)]
        for z in range(NZ):
            window.append(h(z + 1))
            lo, mid, hi = window[-3:]
            if backward:
                lo, hi = hi, lo
            code = m[z, r, :]
            emit(z, r, code, jnp.where(bit(code, 16), lo, jnp.where(bit(code, 32), hi, mid)))
        return 0

    lax.fori_loop(0, EXT // ROWS, body, 0)


def build_mask(mask):
    au = lax.axis_index("au")
    n = lax.axis_size("au")
    mask[...] = jnp.ones((EXT, NV), f32)
    lane = lanes(PAD)
    zero = jnp.zeros((PAD, NV), f32)
    one = jnp.ones((PAD, NV), f32)

    @pl.when(au == 0)
    def _():
        mask[0:PAD, :] = zero
        mask[S0 : S0 + PAD, :] = jnp.where(lane < 32, zero, one)

    @pl.when(au == n - 1)
    def _():
        mask[PAD + NU : S0, :] = zero
        mask[EXT - PAD : EXT, :] = jnp.where(lane >= 96, zero, one)


def start_backward(cot, m, out, up, down):
    def body(z, _):
        code = m[z]
        out[z] = plane_sweeps(kept_of(cot[z], code), code, True)
        return 0

    lax.fori_loop(0, NZ, body, 0)
    up[...] = out[NZ - 2 : NZ]
    down[...] = out[0:1]


def first_kernel(cot, top, bot, dtop, dbot, vst, m, cote, out, up, down):
    v = lax.axis_index("vert")

    def write(z, r, val):
        cote[z, pl.ds(r, val.shape[0]), :] = val

    assemble(
        lambda z, r, n: cot[z, pl.ds(r, n), :],
        (lambda z: top[z], lambda z: dtop[z]),
        (lambda z: bot[z], lambda z: dbot[z]),
        lambda p: vst[p],
        write,
        v,
    )
    start_backward(cote, m.at[0], out, up, down)


def hat_kernel(cote, g, below, above, m, out, up, down, hat, mask):
    build_mask(mask)

    def emit(z, r, code, value):
        hat[z, r, :] = (cote[z, r, :] - value) * mask[r, :]

    depth_sweep(g, below, above, m.at[0], True, emit)

    def body(z, _):
        out[z] = plane_sweeps(hat[z], m[0, z], False)
        return 0

    lax.fori_loop(0, NZ, body, 0)
    up[...] = out[NZ - 1 : NZ]
    down[...] = out[0:2]


def next_kernel(cote, g, below, above, m1, m0, cot2, out, up, down, mask):
    build_mask(mask)

    def emit(z, r, code, value):
        cot2[z, r, :] = (kept_of(cote[z, r, :], code) + value) * mask[r, :]

    depth_sweep(g, below, above, m1.at[0], False, emit)
    start_backward(cot2, m0.at[0], out, up, down)


def last_kernel(cote, g, below, above, m, out, full):
    v = lax.axis_index("vert")

    def emit(z, r, code, value):
        full[z, r, :] = kept_of(cote[z, r, :], code) + value

    depth_sweep(g, below, above, m.at[0], False, emit)
    lane = lanes(32)
    edge = jnp.where(v == 0, lane, NV - 1 - lane) >= NV - 8

    def body(z, _):
        strip = full[z, S0 + PAD : S0 + PAD + 32, :]
        for k in range(4):
            main = full[z, PAD + 32 * k : PAD + 32 * k + 32, :]
            out[z, 32 * k : 32 * k + 32, :] = jnp.where(edge, rot(strip, -(32 * k + 16)), main)
        return 0

    lax.fori_loop(0, NZ, body, 0)


VM = pl.BlockSpec(memory_space=pltpu.VMEM)
SM = pl.BlockSpec(memory_space=pltpu.SMEM)


def call(kernel, outs, *args, scratch=(), scalars=0, whole=(), bytes_accessed=1 << 20):
    def spec(i, a):
        if i < scalars:
            return SM
        if i in whole:
            which = whole[i]
            return pl.BlockSpec((1,) + a.shape[1:], lambda *_: (which,) + (0,) * (a.ndim - 1))
        return VM

    return pl.pallas_call(
        kernel,
        grid=(1,) if whole else (),
        out_shape=[jax.ShapeDtypeStruct(s, d) for s, d in outs],
        in_specs=[spec(i, a) for i, a in enumerate(args)],
        out_specs=[VM] * len(outs),
        scratch_shapes=[pltpu.VMEM(s, f32) for s in scratch],
        cost_estimate=pl.CostEstimate(flops=0, bytes_accessed=bytes_accessed, transcendentals=0),
        compiler_params=pltpu.CompilerParams(vmem_limit_bytes=40 << 20),
    )(*args)


def line(n, step):
    return [(i, i + step) for i in range(n) if 0 <= i + step < n]


def swap(x):
    return lax.ppermute(x, "vert", [(0, 1), (1, 0)])


def beside(top, bot):
    n = lax.axis_size("au")
    from_above = lax.ppermute(bot, "au", line(n, 1))
    from_below = lax.ppermute(top, "au", line(n, -1))
    return from_above, from_below


def diagonal(top, bot):
    n = lax.axis_size("au")
    perm = lambda step: [(2 * a + v, 2 * b + 1 - v) for a, b in line(n, step) for v in range(2)]
    from_above = lax.ppermute(bot, ("au", "vert"), perm(1))
    from_below = lax.ppermute(top, ("au", "vert"), perm(-1))
    return from_above, from_below


def stacked(up, down):
    n = lax.axis_size("depth")
    return lax.ppermute(up, "depth", line(n, 1)), lax.ppermute(down, "depth", line(n, -1))


def per_device(density, image, rows, cols, code, lim):
    depth = lax.axis_size("depth")
    delta = OPTICAL / (NZ * depth)
    i32 = jnp.int32
    vol = ((NZ, NU, NV), f32)
    strip = (NZ // 2, 32, NV)
    plane = lambda n: ((n, EXT, NV), f32)
    top, bot, vst = call(
        pack_density_kernel,
        [((NZ, SHEAR, NV), f32), ((NZ, SHEAR, NV), f32), (strip, f32)],
        density,
    )
    vst = swap(vst)
    top, bot = beside(top, bot)
    ktop, kbot, kvst = call(
        pack_code_kernel,
        [((4, NZ, PAD, NV), i32), ((4, NZ, PAD, NV), i32), ((4,) + strip, i32)],
        code,
        lim,
    )
    g, block = call(
        functools.partial(ray_kernel, delta),
        [((2, NZ, NU, NV), f32), ((NU // 8, 4, 8, NV), f32)],
        rows, cols, density, top, bot, vst,
        scratch=[(NZ, NU + 2 * SHEAR, NV)],
        scalars=2,
    )
    kvst = swap(kvst)
    (ktop1, kbot1), (ktop2, kbot2) = beside(ktop, kbot), diagonal(ktop, kbot)
    spread = lax.all_to_all(block, "depth", 0, 0, tiled=True)
    (far,) = call(functools.partial(scan_kernel, depth), [((depth, 4, 8, NV), f32)], spread)
    far = lax.all_to_all(far, "depth", 0, 0, tiled=True)
    (m,) = call(
        code_kernel, [((2, NZ, EXT, NV), i32)], code, lim, ktop1, kbot1, ktop2, kbot2, kvst
    )
    vg, top, bot, vst = call(
        grad_kernel,
        [((2, NZ, NU, NV), f32), ((NZ, SHEAR, NV), f32), ((NZ, SHEAR, NV), f32), (strip, f32)],
        g, block, far, image,
    )
    vst = swap(vst)
    top, bot = beside(top, bot)
    cot, top, bot, vst = call(
        cotangent_kernel,
        [vol, ((NZ, PAD, NV), f32), ((NZ, PAD, NV), f32), (strip, f32)],
        rows, cols, vg, top, bot, vst,
        scratch=[(NZ, NU + 2 * SHEAR, NV)],
        scalars=2,
    )
    vst = swap(vst)
    (top1, bot1), (top2, bot2) = beside(top, bot), diagonal(top, bot)
    cote, g, up, down = call(
        first_kernel, [plane(NZ), plane(NZ), plane(2), plane(1)],
        cot, top1, bot1, top2, bot2, vst, m, whole={6: 1},
    )
    for s in (1, 0):
        below, above = stacked(up, down)
        g, up, down = call(
            hat_kernel, [plane(NZ), plane(1), plane(2)], cote, g, below, above, m,
            scratch=[(NZ, EXT, NV), (EXT, NV)], whole={4: s},
        )
        below, above = stacked(up, down)
        if s == 1:
            cote, g, up, down = call(
                next_kernel, [plane(NZ), plane(NZ), plane(2), plane(1)],
                cote, g, below, above, m, m,
                scratch=[(EXT, NV)], whole={4: 1, 5: 0},
            )
    (out,) = call(
        last_kernel, [vol], cote, g, below, above, m,
        scratch=[(NZ, EXT, NV)], whole={4: 0},
    )
    return out


def solution(mesh):
    placed = (
        P("depth", "au", "vert"),
        P(None, "au", "vert"),
        P("depth"),
        P("depth"),
        P(None, "depth", "au", "vert"),
        P(None, "depth", "au", "vert"),
    )
    return jax.shard_map(
        per_device, mesh=mesh, in_specs=placed, out_specs=P("depth", "au", "vert"), check_vma=False
    )
```
